512 devices in a mesh: gx: 16 (over y, x_lo, core), gy: 32 (over z, x_hi).
Axes of the slice: x: 4 (x_hi: 2, x_lo: 2; x = x_hi * 2 + x_lo), y: 4, z: 16, core: 2. Of those that a mesh axis runs over, the one named last changes fastest.
Arguments:
- site_tensors: bfloat16 [128, 64, 256, 256], P('gx', 'gy'), may hold values from -6 to 6
- test_matrix: bfloat16 [128, 64, 16, 256], P('gx', 'gy'), may hold values from -0.375 to 0.375
Outputs:
- coarse: bfloat16 [64, 64, 256, 256], P('gx', 'gy')
- log_norm: float32 [64, 64], P('gx', 'gy')
- trace: float32 [64, 64], P('gx', 'gy')
The draws below stay inside these ranges and needn't reach their ends.
All inputs are finite; a program needn't handle non-finite values.
Results may differ from the reference program's by a relative error of at most 0.0086.
Values may be sent and summed in bfloat16 or wider, within the bound.
No kernel may reach another device: no remote copies, remote signals or barrier semaphores. Data moves between devices by JAX's collectives and lax.ppermute only.
A program may use at most 64 MiB of HBM per device.

```python
import jax
import jax.numpy as jnp
from jax import lax

CHI = 16
NX = 128
NY = 64


def level_of(key, shape, split, least, high):
    factor_of, own = 1.0, jax.random.fold_in(key, 6)
    for position, parts in split:
        steps = jnp.exp(jax.random.uniform(jax.random.fold_in(own, position), (parts,), jnp.float32, least / len(split), high / len(split)))
        factor_of = factor_of * jnp.repeat(steps, shape[position] // parts).reshape([-1 if axis == position else 1 for axis in range(len(shape))])
    return factor_of


def gaussian(own_key, dims, deviation, limit, pieces=(), kind=jnp.bfloat16):
    drawn = jax.random.normal(own_key, dims, jnp.float32) * deviation
    if len(pieces) > 0:
        drawn = level_of(own_key, dims, pieces, -0.22, 0.18) * drawn
    return jnp.clip(drawn, min=-limit, max=limit).astype(kind)


def setup_inputs(seed: int = 0) -> dict:
    arg_keys = jax.random.split(jax.random.key(seed), 3)
    site_tensors = gaussian(arg_keys[0], (NX, NY, CHI * CHI, CHI * CHI), 1.0, 6.0, ((0, 16), (1, 32)))
    test_matrix = gaussian(arg_keys[1], (NX, NY, CHI, CHI * CHI), (CHI * CHI) ** -0.5, 0.375, ((0, 16), (1, 32)))
    return dict(site_tensors=site_tensors, test_matrix=test_matrix)


def split_sites(tensors, tests):
    wide = tensors.astype(jnp.float32)
    sketch = jnp.einsum('sij,skj->sik', wide, tests.astype(jnp.float32), precision=lax.Precision.HIGHEST)
    gram_matrix = jnp.einsum('sik,sil->skl', sketch, sketch, precision=lax.Precision.HIGHEST)
    lower_factor = jnp.linalg.cholesky(gram_matrix)
    basis = jax.scipy.linalg.solve_triangular(lower_factor, jnp.swapaxes(sketch, 1, 2), lower=True).astype(jnp.bfloat16)
    second = jnp.einsum('ski,sij->skj', basis.astype(jnp.float32), wide, precision=lax.Precision.HIGHEST).astype(jnp.bfloat16)
    return jnp.stack([basis, second], axis=1)

def pick_sites(halves):
    rows = halves.shape[1]
    paired = halves.reshape(halves.shape[0] // 2, 2, rows, 2, CHI, CHI * CHI)
    odd_rows = (jnp.arange(rows) % 2 == 1)[None, :, None, None, None]
    return jnp.where(odd_rows, paired[:, 1], paired[:, 0])

def contract_sites(first, second, third, fourth):
    count = first.shape[0]
    north_east = first[:, 0].reshape(count, CHI, CHI, CHI).astype(jnp.float32)
    north_west = second[:, 0].reshape(count, CHI, CHI, CHI).astype(jnp.float32)
    south_east = third[:, 1].reshape(count, CHI, CHI, CHI).astype(jnp.float32)
    south_west = fourth[:, 1].reshape(count, CHI, CHI, CHI).astype(jnp.float32)
    pair_low = jnp.einsum('naur,nbvr->nabuv', north_east, north_west, precision=lax.Precision.HIGHEST).astype(jnp.bfloat16)
    pair_high = jnp.einsum('ncru,nevr->nceuv', south_east, south_west, precision=lax.Precision.HIGHEST).astype(jnp.bfloat16)
    pair_low = pair_low.reshape(count, CHI * CHI, CHI * CHI).astype(jnp.float32)
    pair_high = pair_high.reshape(count, CHI * CHI, CHI * CHI).astype(jnp.float32)
    raw = jnp.einsum('nij,nkj->nik', pair_low, pair_high, precision=lax.Precision.HIGHEST)
    squares = lax.optimization_barrier(jnp.sum(raw * raw, axis=(1, 2)))
    norm_value = jnp.sqrt(squares + 1e-06)
    identity = jnp.eye(CHI, dtype=jnp.float32)
    trace_mask = identity[:, None, None, :] * identity[None, :, :, None]
    traced = lax.optimization_barrier(jnp.sum(raw.reshape(count, CHI, CHI, CHI, CHI) * trace_mask[None], axis=(1, 2, 3, 4)))
    coarse = (CHI * CHI * raw / norm_value[:, None, None]).astype(jnp.bfloat16)
    return (coarse, jnp.log(norm_value), CHI * traced / norm_value)

def reference(site_tensors, test_matrix):

    def split_column(packed):
        column_tensors, column_tests = packed
        return split_sites(column_tensors, column_tests)
    halves = lax.map(split_column, (site_tensors, test_matrix))
    right_sites = jnp.roll(halves, -1, axis=0)
    upper_sites = jnp.roll(halves, -1, axis=1)
    corner_sites = jnp.roll(right_sites, -1, axis=1)
    picked = (pick_sites(halves), pick_sites(right_sites), pick_sites(upper_sites), pick_sites(corner_sites))

    def contract_column(packed):
        return contract_sites(packed[0], packed[1], packed[2], packed[3])
    coarse, log_norm, trace = lax.map(contract_column, picked)
    return (coarse, log_norm, trace)
```

```python
import jax
import jax.numpy as jnp
from jax import lax
from jax.experimental import pallas as pl
from jax.experimental.pallas import tpu as pltpu
from jax.sharding import PartitionSpec as P

CHI = 16
WIDE = CHI * CHI
HALF = 128
NT = (((1,), (1,)), ((), ()))
NN = (((1,), (0,)), ((), ()))


def dot(a, b, dims=NN):
    return lax.dot_general(a, b, dims, preferred_element_type=jnp.float32)


def split_kernel(columns, rows, tensors, tests, basis, second, above, right, corner, vm, vt, work, sem_m, sem_t):
    sites = columns * rows
    place = [(s // rows, s % rows) for s in range(sites)]
    test_copy = pltpu.make_async_copy(tests, vt, sem_t)
    test_copy.start()
    copies = [pltpu.make_async_copy(tensors.at[x, y], vm.at[s], sem_m.at[s]) for s, (x, y) in enumerate(place)]
    for copy in copies:
        copy.start()
    test_copy.wait()
    for s, (x, y) in enumerate(place):
        copies[s].wait()
        sketch = dot(vt[x, y], vm[s], NT)
        for h in range(2):
            work[h, pl.ds(s, CHI, stride=sites), :] = sketch[:, h * HALF : (h + 1) * HALF]

    def line(h, k):
        return work[h, k * sites : (k + 1) * sites, :]

    def inner(i, j):
        parts = line(0, i) * line(0, j) + line(1, i) * line(1, j)
        return jnp.broadcast_to(jnp.sum(parts, axis=1, keepdims=True), (sites, HALF))

    gram = {(i, j): inner(i, j) for j in range(CHI) for i in range(j, CHI)}
    for k in range(CHI):
        scale = lax.rsqrt(gram[k, k])
        lower = {i: gram[i, k] * scale for i in range(k + 1, CHI)}
        for i in range(k + 1, CHI):
            for j in range(k + 1, i + 1):
                gram[i, j] = gram[i, j] - lower[i] * lower[j]
        for h in range(2):
            row = line(h, k) * scale
            work[h, k * sites : (k + 1) * sites, :] = row
            for i in range(k + 1, CHI):
                work[h, i * sites : (i + 1) * sites, :] = line(h, i) - lower[i] * row
    for s, (x, y) in enumerate(place):
        rows_k = [work[h, pl.ds(s, CHI, stride=sites), :] for h in range(2)]
        q = jnp.concatenate(rows_k, axis=1).astype(jnp.bfloat16)
        rest = dot(q, vm[s]).astype(jnp.bfloat16)
        if y == 1 and x == 0:
            right[0] = q
        else:
            basis[x, y] = q
        if y == 1:
            second[x] = rest
        elif x == 0:
            corner[0] = rest
        else:
            above[x - 1] = rest


def split_block(tensors, tests):
    columns, rows = tensors.shape[0], tensors.shape[1]
    sites = columns * rows
    shapes = [(columns, rows), (columns,), (columns - 1,), (1,), (1,)]
    anywhere = pl.BlockSpec(memory_space=pl.ANY)
    return pl.pallas_call(
        lambda *refs: split_kernel(columns, rows, *refs),
        out_shape=[pltpu.VMEM(shape + (CHI, WIDE), jnp.bfloat16) for shape in shapes],
        in_specs=[anywhere] * 2,
        out_specs=[pl.BlockSpec(memory_space=pltpu.VMEM)] * 5,
        scratch_shapes=[
            pltpu.VMEM((sites, WIDE, WIDE), jnp.bfloat16),
            pltpu.VMEM((columns, rows, CHI, WIDE), jnp.bfloat16),
            pltpu.VMEM((2, CHI * sites, HALF), jnp.float32),
            pltpu.SemaphoreType.DMA((sites,)),
            pltpu.SemaphoreType.DMA,
        ],
        name="split",
    )(tensors, tests)


def widen(half, pick, tile):
    spread = jnp.broadcast_to(half.astype(jnp.float32)[:, None, :], (CHI, CHI, WIDE)).reshape(WIDE, WIDE)
    spread = jnp.where(pick, spread, 0.0).astype(jnp.bfloat16)
    return dot(spread, tile).astype(jnp.bfloat16)


def pair_up(wide, other, own, out):
    left = jnp.concatenate([other[:, :HALF], other[:, HALF:]], axis=0)
    for a in range(0, CHI, 2):
        blocks = []
        for step in range(2):
            piece = wide[(a + step) * CHI : (a + step + 1) * CHI, :]
            zero = jnp.zeros_like(piece)
            blocks.append(jnp.concatenate([jnp.where(own[v], piece, zero) for v in range(8)], axis=0))
        got = dot(left, jnp.concatenate(blocks, axis=1)).astype(jnp.bfloat16)
        for step in range(2):
            base = (a + step) * CHI
            for h in range(2):
                out[base : base + CHI, h * HALF : (h + 1) * HALF] = got[
                    h * CHI : (h + 1) * CHI, step * HALF : (step + 1) * HALF
                ]


def contract_kernel(count, row, *refs):
    coarse, logs, traces, low, high, done, sem = refs[-7:]
    if row:
        basis, above, right, corner, _, kept_logs, kept_traces = refs[:-7]
    else:
        basis, second = refs[:-7]

    def corners(p):
        if not row:
            return basis[2 * p, 0], basis[2 * p + 1, 0], second[2 * p], second[2 * p + 1]
        if p < count - 1:
            return basis[2 * p + 1, 1], basis[2 * p + 2, 1], above[2 * p], above[2 * p + 1]
        return basis[2 * p + 1, 1], right[0], above[2 * p], corner[0]

    iota = lambda shape, axis: lax.broadcasted_iota(jnp.int32, shape, axis)
    r, c = iota((WIDE, WIDE), 0), iota((WIDE, WIDE), 1)
    pick_minor = (c % CHI) == (r % CHI)
    pick_major = (c // CHI) == (r % CHI)
    rt, ct = iota((WIDE, HALF), 0), iota((WIDE, HALF), 1)
    tile_major = ((rt // CHI) == (ct % CHI)).astype(jnp.float32).astype(jnp.bfloat16)
    tile_minor = ((rt % CHI) == (ct % CHI)).astype(jnp.float32).astype(jnp.bfloat16)
    lane = iota((CHI, HALF), 1)
    own = [(lane // CHI) == v for v in range(8)]
    crossed = ((c // CHI) == (r % CHI)) & ((c % CHI) == (r // CHI))
    small_row, small_col = iota((2, count), 0), iota((2, count), 1)
    if row:
        all_logs, all_traces = kept_logs[...], kept_traces[...]
    else:
        all_logs = all_traces = jnp.zeros((2, count), jnp.float32)
    copies = []
    for p in range(count):
        north_east, north_west, south_east, south_west = corners(p)
        pair_up(widen(north_east, pick_minor, tile_major), north_west, own, low.at[p % 2])
        pair_up(widen(south_east, pick_major, tile_minor), south_west, own, high.at[p % 2])
        raw = dot(low[p % 2], high[p % 2], NT)
        square = jnp.sum(jnp.sum(raw * raw, axis=0, keepdims=True), axis=1, keepdims=True) + 1e-06
        scale = lax.rsqrt(square)
        done[p] = (raw * (CHI * CHI * scale)).astype(jnp.bfloat16)
        copy = pltpu.make_async_copy(done.at[p], coarse.at[p, row], sem.at[p])
        copy.start()
        copies.append(copy)
        diagonal = jnp.where(crossed, raw, 0.0)
        traced = jnp.sum(jnp.sum(diagonal, axis=0, keepdims=True), axis=1, keepdims=True)
        here = (small_row == row) & (small_col == p)
        all_logs = jnp.where(here, 0.5 * jnp.log(square), all_logs)
        all_traces = jnp.where(here, CHI * traced * scale, all_traces)
    logs[...] = all_logs
    traces[...] = all_traces
    for copy in copies:
        copy.wait()


def contract(row, halves, before):
    count = halves[0].shape[0] // 2
    anywhere = pl.BlockSpec(memory_space=pl.ANY)
    vmem = pl.BlockSpec(memory_space=pltpu.VMEM)
    small = jax.ShapeDtypeStruct if row else pltpu.VMEM
    before = before and (before[0],) + tuple(pltpu.with_memory_space_constraint(x, pltpu.VMEM) for x in before[1:])
    return pl.pallas_call(
        lambda *refs: contract_kernel(count, row, *refs),
        out_shape=(
            jax.ShapeDtypeStruct((count, 2, WIDE, WIDE), jnp.bfloat16),
            small((2, count), jnp.float32),
            small((2, count), jnp.float32),
        ),
        in_specs=[vmem] * len(halves) + [anywhere, vmem, vmem][: len(before)],
        out_specs=(anywhere, vmem, vmem),
        input_output_aliases={len(halves): 0} if before else {},
        scratch_shapes=[
            pltpu.VMEM((2, WIDE, WIDE), jnp.bfloat16),
            pltpu.VMEM((2, WIDE, WIDE), jnp.bfloat16),
            pltpu.VMEM((count, WIDE, WIDE), jnp.bfloat16),
            pltpu.SemaphoreType.DMA((count,)),
        ],
        name="contract",
    )(*[pltpu.with_memory_space_constraint(half, pltpu.VMEM) for half in halves], *before)


def pull(x, dx, dy):
    nx, ny = lax.axis_size("gx"), lax.axis_size("gy")
    pairs = [
        (i * ny + j, (i - dx) % nx * ny + (j - dy) % ny) for i in range(nx) for j in range(ny)
    ]
    return lax.ppermute(x, ("gx", "gy"), pairs)


def body(site_tensors, test_matrix):
    basis, second, above, right, corner = split_block(site_tensors, test_matrix)
    above = pull(above, 0, 1)
    right = pull(right, 1, 0)
    corner = pull(corner, 1, 1)
    before = contract(0, (basis, second), ())
    coarse, log_norm, trace = contract(1, (basis, above, right, corner), before)
    return coarse, log_norm.T, trace.T


def solution(mesh):
    in_specs = (P("gx", "gy", None, None), P("gx", "gy", None, None))
    out_specs = (P("gx", "gy", None, None), P("gx", "gy"), P("gx", "gy"))
    return jax.shard_map(body, mesh=mesh, in_specs=in_specs, out_specs=out_specs, check_vma=False)
```

```python
import jax
import jax.numpy as jnp
from jax import lax
from jax.experimental import pallas as pl
from jax.experimental.pallas import tpu as pltpu
from jax.sharding import PartitionSpec as P

CHI = 16
WIDE = CHI * CHI
HALF = 128
NT = (((1,), (1,)), ((), ()))
NN = (((1,), (0,)), ((), ()))


ANY = pl.BlockSpec(memory_space=pl.ANY)
VMEM = pl.BlockSpec(memory_space=pltpu.VMEM)
GRANT = pltpu.CompilerParams(vmem_limit_bytes=32 << 20)


def near(*arrays):
    return [pltpu.with_memory_space_constraint(x, pltpu.VMEM) for x in arrays]


def dot(a, b, dims=NN):
    return lax.dot_general(a, b, dims, preferred_element_type=jnp.float32)


def split_sites(sources, slots, work):
    count = len(sources)
    for s, (test, tensor) in enumerate(sources):
        sketch = dot(test[...], tensor[...], NT)
        for slot in range(s, slots, count):
            for h in range(2):
                work[h, pl.ds(slot, CHI, stride=slots), :] = sketch[:, h * HALF : (h + 1) * HALF]

    def line(h, k):
        return work[h, k * slots : (k + 1) * slots, :]

    def inner(i, j):
        parts = line(0, i) * line(0, j) + line(1, i) * line(1, j)
        return jnp.broadcast_to(jnp.sum(parts, axis=1, keepdims=True), (slots, HALF))

    gram = {(i, j): inner(i, j) for j in range(CHI) for i in range(j, CHI)}
    for k in range(CHI):
        scale = lax.rsqrt(gram[k, k])
        lower = {i: gram[i, k] * scale for i in range(k + 1, CHI)}
        for i in range(k + 1, CHI):
            for j in range(k + 1, i + 1):
                gram[i, j] = gram[i, j] - lower[i] * lower[j]
        for h in range(2):
            row = line(h, k) * scale
            work[h, k * slots : (k + 1) * slots, :] = row
            for i in range(k + 1, CHI):
                work[h, i * slots : (i + 1) * slots, :] = line(h, i) - lower[i] * row
    for s, (_, tensor) in enumerate(sources):
        halves = [work[h, pl.ds(s, CHI, stride=slots), :] for h in range(2)]
        basis = jnp.concatenate(halves, axis=1).astype(jnp.bfloat16)
        yield s, basis, dot(basis, tensor[...]).astype(jnp.bfloat16)


def left_kernel(columns, rows, tensors, tests, leftmost, vm, vt, work, sem):
    copies = []
    for x in range(columns):
        copies.append(pltpu.make_async_copy(tests.at[x], vt.at[x], sem.at[0, x]))
        copies.append(pltpu.make_async_copy(tensors.at[x], vm.at[x], sem.at[1, x]))
    for copy in copies:
        copy.start()
    for copy in copies[:2]:
        copy.wait()
    for y, basis, second in split_sites([(vt.at[0, y], vm.at[0, y]) for y in range(rows)], 8, work):
        leftmost[1 - y] = basis if y == 1 else second
    for copy in copies[2:]:
        copy.wait()


def split_kernel(columns, rows, tensors, tests, basis, second, lowest, work):
    place = [(x, y) for x in range(columns) for y in range(rows)]
    for s, one, other in split_sites([(tests.at[x, y], tensors.at[x, y]) for x, y in place], len(place), work):
        x, y = place[s]
        basis[x, y] = one
        if y == 1:
            second[x] = other
        elif x > 0:
            lowest[x - 1] = other


def split_left(tensors, tests):
    columns, rows = tensors.shape[0], tensors.shape[1]
    return pl.pallas_call(
        lambda *refs: left_kernel(columns, rows, *refs),
        out_shape=[
            pltpu.VMEM((2, CHI, WIDE), jnp.bfloat16),
            pltpu.VMEM(tensors.shape, tensors.dtype),
            pltpu.VMEM(tests.shape, tests.dtype),
        ],
        in_specs=[ANY] * 2,
        out_specs=[VMEM] * 3,
        scratch_shapes=[pltpu.VMEM((2, CHI * 8, HALF), jnp.float32), pltpu.SemaphoreType.DMA((2, columns))],
        compiler_params=GRANT,
        name="split_left",
    )(*[pltpu.with_memory_space_constraint(x, pltpu.HBM) for x in (tensors, tests)])


def split_block(tensors, tests):
    columns, rows = tensors.shape[0], tensors.shape[1]
    shapes = [(columns, rows), (columns,), (columns,)]
    return pl.pallas_call(
        lambda *refs: split_kernel(columns, rows, *refs),
        out_shape=[pltpu.VMEM(shape + (CHI, WIDE), jnp.bfloat16) for shape in shapes],
        in_specs=[VMEM] * 2,
        out_specs=[VMEM] * 3,
        scratch_shapes=[pltpu.VMEM((2, CHI * columns * rows, HALF), jnp.float32)],
        compiler_params=GRANT,
        name="split",
    )(*near(tensors, tests))


def widen(half, pick, tile):
    spread = jnp.broadcast_to(half.astype(jnp.float32)[:, None, :], (CHI, CHI, WIDE)).reshape(WIDE, WIDE)
    spread = jnp.where(pick, spread, 0.0).astype(jnp.bfloat16)
    return dot(spread, tile).astype(jnp.bfloat16)


def pair_up(wide, other, own, out):
    left = jnp.concatenate([other[:, :HALF], other[:, HALF:]], axis=0)
    for a in range(0, CHI, 2):
        blocks = []
        for step in range(2):
            piece = wide[(a + step) * CHI : (a + step + 1) * CHI, :]
            zero = jnp.zeros_like(piece)
            blocks.append(jnp.concatenate([jnp.where(own[v], piece, zero) for v in range(8)], axis=0))
        got = dot(left, jnp.concatenate(blocks, axis=1)).astype(jnp.bfloat16)
        for step in range(2):
            base = (a + step) * CHI
            for h in range(2):
                out[base : base + CHI, h * HALF : (h + 1) * HALF] = got[
                    h * CHI : (h + 1) * CHI, step * HALF : (step + 1) * HALF
                ]


def patterns():
    iota = lambda shape, axis: lax.broadcasted_iota(jnp.int32, shape, axis)
    r, c = iota((WIDE, WIDE), 0), iota((WIDE, WIDE), 1)
    rt, ct = iota((WIDE, HALF), 0), iota((WIDE, HALF), 1)
    lane = iota((CHI, HALF), 1)
    return dict(
        pick_minor=(c % CHI) == (r % CHI),
        pick_major=(c // CHI) == (r % CHI),
        tile_major=((rt // CHI) == (ct % CHI)).astype(jnp.float32).astype(jnp.bfloat16),
        tile_minor=((rt % CHI) == (ct % CHI)).astype(jnp.float32).astype(jnp.bfloat16),
        own=[(lane // CHI) == v for v in range(8)],
        crossed=((c // CHI) == (r % CHI)) & ((c % CHI) == (r // CHI)),
        small=(iota((8, HALF), 0), iota((8, HALF), 1)),
    )


def contract_row(row, count, corners, coarse, stats, low, high, done, sem):
    at = patterns()
    rows, lanes = at["small"]
    copies = []
    for p in range(count):
        north_east, north_west, south_east, south_west = corners(p)
        pair_up(widen(north_east, at["pick_minor"], at["tile_major"]), north_west, at["own"], low.at[p % 2])
        pair_up(widen(south_east, at["pick_major"], at["tile_minor"]), south_west, at["own"], high.at[p % 2])
        raw = dot(low[p % 2], high[p % 2], NT)
        square = jnp.sum(jnp.sum(raw * raw, axis=0, keepdims=True), axis=1, keepdims=True) + 1e-06
        scale = lax.rsqrt(square)
        done[p] = (raw * (CHI * CHI * scale)).astype(jnp.bfloat16)
        copy = pltpu.make_async_copy(done.at[p], coarse.at[p, row], sem.at[p])
        copy.start()
        copies.append(copy)
        diagonal = jnp.where(at["crossed"], raw, 0.0)
        traced = jnp.sum(jnp.sum(diagonal, axis=0, keepdims=True), axis=1, keepdims=True)
        stats = jnp.where((rows == row) & (lanes == p), 0.5 * jnp.log(square), stats)
        stats = jnp.where((rows == 2 + row) & (lanes == p), CHI * traced * scale, stats)
    return stats, copies


def inner_kernel(count, kind, now, basis, second, *refs):
    stats_in = None
    if kind == "ahead":
        coarse, stats, low, high, done, sem = refs
    else:
        _, stats_in, coarse, stats, low, high, done, sem = refs

    def corners(p):
        return basis[2 * p, 0], basis[2 * p + 1, 0], second[2 * p], second[2 * p + 1]

    here = now()

    @pl.when(here)
    def _():
        got, copies = contract_row(0, count, corners, coarse, jnp.zeros((8, HALF), jnp.float32), low, high, done, sem)
        stats[...] = got
        for copy in copies:
            copy.wait()

    @pl.when(jnp.logical_not(here))
    def _():
        stats[...] = jnp.zeros((8, HALF), jnp.float32) if stats_in is None else stats_in[...]


def outer_kernel(count, now, alone, basis, above, leftmost, leftmost_alone, stats_in, *refs):
    coarse, logs, traces, lowest, low, high, done, sem, vs, sem_s = refs[-10:]
    apart = alone()
    right = jnp.where(jnp.full((CHI, WIDE), apart), leftmost_alone[0].astype(jnp.float32), leftmost[0].astype(jnp.float32))
    right = right.astype(jnp.bfloat16)

    @pl.when(apart)
    def _():
        lowest[2 * count - 1] = leftmost_alone[1]

    def corners(p):
        return basis[2 * p + 1, 1], basis[2 * p + 2, 1] if p < count - 1 else right, above[2 * p], above[2 * p + 1]

    @pl.when(now())
    def _():
        stats, copies = contract_row(1, count, corners, coarse, stats_in[...], low, high, done, sem)
        vs[0] = stats[0:2, :count]
        vs[1] = stats[2:4, :count]
        small = [pltpu.make_async_copy(vs.at[0], logs, sem_s.at[0]), pltpu.make_async_copy(vs.at[1], traces, sem_s.at[1])]
        for copy in small:
            copy.start()
        for copy in copies + small:
            copy.wait()


def scratch(count):
    return [
        pltpu.VMEM((2, WIDE, WIDE), jnp.bfloat16),
        pltpu.VMEM((2, WIDE, WIDE), jnp.bfloat16),
        pltpu.VMEM((count, WIDE, WIDE), jnp.bfloat16),
        pltpu.SemaphoreType.DMA((count,)),
    ]


def whole(count):
    return jax.ShapeDtypeStruct((count, 2, WIDE, WIDE), jnp.bfloat16)


def inner(kind, now, basis, second, *before):
    count = second.shape[0] // 2
    return pl.pallas_call(
        lambda *refs: inner_kernel(count, kind, now, *refs),
        out_shape=(whole(count), pltpu.VMEM((8, HALF), jnp.float32)),
        in_specs=[VMEM, VMEM, ANY, VMEM][: 2 + len(before)],
        out_specs=(ANY, VMEM),
        input_output_aliases={2: 0} if before else {},
        scratch_shapes=scratch(count),
        compiler_params=GRANT,
        name="inner_" + kind,
    )(*near(basis, second), *before[:1], *near(*before[1:]))


def pack(lowest, right, own, stats):
    def kernel(lowest_in, right_in, own_in, stats_in, lowest_out, own_out, stats_out):
        lowest_out[lowest.shape[0] - 1] = right_in[1]

    return pl.pallas_call(
        kernel,
        out_shape=[pltpu.VMEM(x.shape, x.dtype) for x in (lowest, own, stats)],
        in_specs=[VMEM] * 4,
        out_specs=[VMEM] * 3,
        input_output_aliases={0: 0, 2: 1, 3: 2},
        compiler_params=GRANT,
        name="pack",
    )(*near(lowest, right, own, stats))


def outer(now, alone, basis, above, leftmost, leftmost_alone, stats, lowest, coarse, *small):
    count = above.shape[0] // 2
    shape = jax.ShapeDtypeStruct((2, count), jnp.float32)
    return pl.pallas_call(
        lambda *refs: outer_kernel(count, now, alone, *refs),
        out_shape=(whole(count), shape, shape, pltpu.VMEM(lowest.shape, lowest.dtype)),
        in_specs=[VMEM] * 6 + [ANY] * (1 + len(small)),
        out_specs=(ANY, ANY, ANY, VMEM),
        input_output_aliases={5: 3, 6: 0} | {7 + k: 1 + k for k in range(len(small))},
        scratch_shapes=scratch(count) + [pltpu.VMEM((2, 2, count), jnp.float32), pltpu.SemaphoreType.DMA((2,))],
        compiler_params=GRANT,
        name="outer",
    )(*near(basis, above, leftmost, leftmost_alone, stats, lowest), coarse, *small)


def pull(x, dx, dy, takes):
    nx, ny = lax.axis_size("gx"), lax.axis_size("gy")
    pairs = [
        ((g + dx) % nx * ny + (h + dy) % ny, g * ny + h) for g in range(nx) for h in range(ny) if takes(g, h)
    ]
    return lax.ppermute(x, ("gx", "gy"), pairs)


def body(site_tensors, test_matrix):
    columns, rows = lax.axis_size("gx"), lax.axis_size("gy")
    half = 17 if rows > 17 else max(1, rows // 2)
    g = lambda: lax.axis_index("gx")
    h = lambda: lax.axis_index("gy")
    ahead = lambda: (h() == 0) & ((g() == 1) | (g() == columns - 1))
    near_rest = lambda: jnp.logical_not(ahead()) & (h() < half)
    alone = lambda: (g() == 0) & (h() == 0)
    leftmost, tensors, tests = split_left(site_tensors, test_matrix)
    right = pull(leftmost, 1, 0, lambda i, j: (i, j) != (0, 0))
    basis, second, lowest = split_block(tensors, tests)
    coarse, stats = inner("ahead", ahead, basis, second)
    lowest, leftmost, stats = pack(lowest, right, leftmost, stats)
    near_above = pull(lowest, 0, 1, lambda i, j: j < half)
    right_alone = pull(leftmost, 1, 0, lambda i, j: (i, j) == (0, 0))
    coarse, stats = inner("near", near_rest, basis, second, coarse, stats)
    coarse, log_norm, trace, lowest = outer(
        lambda: h() < half, alone, basis, near_above, right, right_alone, stats, lowest, coarse
    )
    far_above = pull(lowest, 0, 1, lambda i, j: j >= half)
    coarse, stats = inner("far", lambda: h() >= half, basis, second, coarse, stats)
    coarse, log_norm, trace, _ = outer(
        lambda: h() >= half, alone, basis, far_above, right, right_alone, stats, lowest, coarse, log_norm, trace
    )
    return coarse, log_norm.T, trace.T


def solution(mesh):
    in_specs = (P("gx", "gy", None, None), P("gx", "gy", None, None))
    out_specs = (P("gx", "gy", None, None), P("gx", "gy"), P("gx", "gy"))
    return jax.shard_map(body, mesh=mesh, in_specs=in_specs, out_specs=out_specs, check_vma=False)
```

```python
import jax
import jax.numpy as jnp
from jax import lax
from jax.experimental import pallas as pl
from jax.experimental.pallas import tpu as pltpu
from jax.sharding import PartitionSpec as P

CHI = 16
WIDE = CHI * CHI
HALF = 128
NT = (((1,), (1,)), ((), ()))
NN = (((1,), (0,)), ((), ()))


ANY = pl.BlockSpec(memory_space=pl.ANY)
VMEM = pl.BlockSpec(memory_space=pltpu.VMEM)
GRANT = pltpu.CompilerParams(vmem_limit_bytes=32 << 20)


def near(*arrays):
    return [pltpu.with_memory_space_constraint(x, pltpu.VMEM) for x in arrays]


def dot(a, b, dims=NN):
    return lax.dot_general(a, b, dims, preferred_element_type=jnp.float32)


def split_sites(sources, slots, work):
    count = len(sources)
    for s, (test, tensor) in enumerate(sources):
        sketch = dot(test[...], tensor[...], NT)
        for slot in range(s, slots, count):
            for h in range(2):
                work[h, pl.ds(slot, CHI, stride=slots), :] = sketch[:, h * HALF : (h + 1) * HALF]

    def line(h, k):
        return work[h, k * slots : (k + 1) * slots, :]

    def inner(i, j):
        parts = line(0, i) * line(0, j) + line(1, i) * line(1, j)
        return jnp.broadcast_to(jnp.sum(parts, axis=1, keepdims=True), (slots, HALF))

    gram = {(i, j): inner(i, j) for j in range(CHI) for i in range(j, CHI)}
    for k in range(CHI):
        scale = lax.rsqrt(gram[k, k])
        lower = {i: gram[i, k] * scale for i in range(k + 1, CHI)}
        for i in range(k + 1, CHI):
            for j in range(k + 1, i + 1):
                gram[i, j] = gram[i, j] - lower[i] * lower[j]
        for h in range(2):
            row = line(h, k) * scale
            work[h, k * slots : (k + 1) * slots, :] = row
            for i in range(k + 1, CHI):
                work[h, i * slots : (i + 1) * slots, :] = line(h, i) - lower[i] * row
    for s, (_, tensor) in enumerate(sources):
        halves = [work[h, pl.ds(s, CHI, stride=slots), :] for h in range(2)]
        basis = jnp.concatenate(halves, axis=1).astype(jnp.bfloat16)
        yield s, basis, dot(basis, tensor[...]).astype(jnp.bfloat16)


def left_kernel(columns, rows, tensors, tests, leftmost, vm, vt, work, sem):
    copies = []
    for x in range(columns):
        copies.append(pltpu.make_async_copy(tests.at[x], vt.at[x], sem.at[0, x]))
        copies.append(pltpu.make_async_copy(tensors.at[x], vm.at[x], sem.at[1, x]))
    for copy in copies:
        copy.start()
    for copy in copies[:2]:
        copy.wait()
    for y, basis, second in split_sites([(vt.at[0, y], vm.at[0, y]) for y in range(rows)], 8, work):
        leftmost[1 - y] = basis if y == 1 else second
    for copy in copies[2:]:
        copy.wait()


def split_kernel(columns, rows, tensors, tests, basis, second, lowest, work):
    place = [(x, y) for x in range(columns) for y in range(rows)]
    for s, one, other in split_sites([(tests.at[x, y], tensors.at[x, y]) for x, y in place], len(place), work):
        x, y = place[s]
        basis[x, y] = one
        if y == 1:
            second[x] = other
        elif x > 0:
            lowest[x - 1] = other


def split_left(tensors, tests):
    columns, rows = tensors.shape[0], tensors.shape[1]
    return pl.pallas_call(
        lambda *refs: left_kernel(columns, rows, *refs),
        out_shape=[
            pltpu.VMEM((2, CHI, WIDE), jnp.bfloat16),
            pltpu.VMEM(tensors.shape, tensors.dtype),
            pltpu.VMEM(tests.shape, tests.dtype),
        ],
        in_specs=[ANY] * 2,
        out_specs=[VMEM] * 3,
        scratch_shapes=[pltpu.VMEM((2, CHI * 8, HALF), jnp.float32), pltpu.SemaphoreType.DMA((2, columns))],
        compiler_params=GRANT,
        name="split_left",
    )(*[pltpu.with_memory_space_constraint(x, pltpu.HBM) for x in (tensors, tests)])


def split_block(tensors, tests):
    columns, rows = tensors.shape[0], tensors.shape[1]
    shapes = [(columns, rows), (columns,), (columns,)]
    return pl.pallas_call(
        lambda *refs: split_kernel(columns, rows, *refs),
        out_shape=[pltpu.VMEM(shape + (CHI, WIDE), jnp.bfloat16) for shape in shapes],
        in_specs=[VMEM] * 2,
        out_specs=[VMEM] * 3,
        scratch_shapes=[pltpu.VMEM((2, CHI * columns * rows, HALF), jnp.float32)],
        compiler_params=GRANT,
        name="split",
    )(*near(tensors, tests))


def widen(half, pick, tile):
    spread = jnp.broadcast_to(half.astype(jnp.float32)[:, None, :], (CHI, CHI, WIDE)).reshape(WIDE, WIDE)
    spread = jnp.where(pick, spread, 0.0).astype(jnp.bfloat16)
    return dot(spread, tile).astype(jnp.bfloat16)


def pair_up(wide, other, own, out):
    left = jnp.concatenate([other[:, :HALF], other[:, HALF:]], axis=0)
    for a in range(0, CHI, 2):
        blocks = []
        for step in range(2):
            piece = wide[(a + step) * CHI : (a + step + 1) * CHI, :]
            zero = jnp.zeros_like(piece)
            blocks.append(jnp.concatenate([jnp.where(own[v], piece, zero) for v in range(8)], axis=0))
        got = dot(left, jnp.concatenate(blocks, axis=1)).astype(jnp.bfloat16)
        for step in range(2):
            base = (a + step) * CHI
            for h in range(2):
                out[base : base + CHI, h * HALF : (h + 1) * HALF] = got[
                    h * CHI : (h + 1) * CHI, step * HALF : (step + 1) * HALF
                ]


def patterns():
    iota = lambda shape, axis: lax.broadcasted_iota(jnp.int32, shape, axis)
    r, c = iota((WIDE, WIDE), 0), iota((WIDE, WIDE), 1)
    rt, ct = iota((WIDE, HALF), 0), iota((WIDE, HALF), 1)
    lane = iota((CHI, HALF), 1)
    return dict(
        pick_minor=(c % CHI) == (r % CHI),
        pick_major=(c // CHI) == (r % CHI),
        tile_major=((rt // CHI) == (ct % CHI)).astype(jnp.float32).astype(jnp.bfloat16),
        tile_minor=((rt % CHI) == (ct % CHI)).astype(jnp.float32).astype(jnp.bfloat16),
        own=[(lane // CHI) == v for v in range(8)],
        crossed=((c // CHI) == (r % CHI)) & ((c % CHI) == (r // CHI)),
        small=(iota((8, HALF), 0), iota((8, HALF), 1)),
    )


def contract_row(row, count, corners, coarse, stats, low, high, done, sem):
    at = patterns()
    rows, lanes = at["small"]
    copies = []
    pairs = []
    for p in range(count):
        north_east, north_west, south_east, south_west = corners(p)
        pairs.append((widen(north_east, at["pick_minor"], at["tile_major"]), north_west, low.at[p]))
        pairs.append((widen(south_east, at["pick_major"], at["tile_minor"]), south_west, high.at[p]))
    for wide, other, out in pairs:
        pair_up(wide, other, at["own"], out)
    products = [dot(low[p], high[p], NT) for p in range(count)]
    for p, raw in enumerate(products):
        square = jnp.sum(jnp.sum(raw * raw, axis=0, keepdims=True), axis=1, keepdims=True) + 1e-06
        scale = lax.rsqrt(square)
        done[p] = (raw * (CHI * CHI * scale)).astype(jnp.bfloat16)
        copy = pltpu.make_async_copy(done.at[p], coarse.at[p, row], sem.at[p])
        copy.start()
        copies.append(copy)
        diagonal = jnp.where(at["crossed"], raw, 0.0)
        traced = jnp.sum(jnp.sum(diagonal, axis=0, keepdims=True), axis=1, keepdims=True)
        stats = jnp.where((rows == row) & (lanes == p), 0.5 * jnp.log(square), stats)
        stats = jnp.where((rows == 2 + row) & (lanes == p), CHI * traced * scale, stats)
    return stats, copies


def inner_kernel(count, kind, now, basis, second, *refs):
    stats_in = None
    if kind == "ahead":
        coarse, stats, low, high, done, sem = refs
    else:
        _, stats_in, coarse, stats, low, high, done, sem = refs

    def corners(p):
        return basis[2 * p, 0], basis[2 * p + 1, 0], second[2 * p], second[2 * p + 1]

    here = now()

    @pl.when(here)
    def _():
        got, copies = contract_row(0, count, corners, coarse, jnp.zeros((8, HALF), jnp.float32), low, high, done, sem)
        stats[...] = got
        for copy in copies:
            copy.wait()

    @pl.when(jnp.logical_not(here))
    def _():
        stats[...] = jnp.zeros((8, HALF), jnp.float32) if stats_in is None else stats_in[...]


def outer_kernel(count, now, basis, above, right, stats_in, *refs):
    coarse, logs, traces, _, low, high, done, sem, vs, sem_s = refs[-10:]

    def corners(p):
        beside = basis[2 * p + 2, 1] if p < count - 1 else right[0]
        return basis[2 * p + 1, 1], beside, above[2 * p], above[2 * p + 1]

    @pl.when(now())
    def _():
        stats, copies = contract_row(1, count, corners, coarse, stats_in[...], low, high, done, sem)
        vs[0] = stats[0:2, :count]
        vs[1] = stats[2:4, :count]
        small = [pltpu.make_async_copy(vs.at[0], logs, sem_s.at[0]), pltpu.make_async_copy(vs.at[1], traces, sem_s.at[1])]
        for copy in small:
            copy.start()
        for copy in copies + small:
            copy.wait()


def scratch(count):
    return [
        pltpu.VMEM((count, WIDE, WIDE), jnp.bfloat16),
        pltpu.VMEM((count, WIDE, WIDE), jnp.bfloat16),
        pltpu.VMEM((count, WIDE, WIDE), jnp.bfloat16),
        pltpu.SemaphoreType.DMA((count,)),
    ]


def whole(count):
    return jax.ShapeDtypeStruct((count, 2, WIDE, WIDE), jnp.bfloat16)


def inner(kind, now, basis, second, *before):
    count = second.shape[0] // 2
    return pl.pallas_call(
        lambda *refs: inner_kernel(count, kind, now, *refs),
        out_shape=(whole(count), pltpu.VMEM((8, HALF), jnp.float32)),
        in_specs=[VMEM, VMEM, ANY, VMEM][: 2 + len(before)],
        out_specs=(ANY, VMEM),
        input_output_aliases={2: 0} if before else {},
        scratch_shapes=scratch(count),
        compiler_params=GRANT,
        name="inner_" + kind,
    )(*near(basis, second), *before[:1], *near(*before[1:]))


def pack(lowest, right, stats):
    def kernel(lowest_in, right_in, stats_in, lowest_out, stats_out):
        lowest_out[lowest.shape[0] - 1] = right_in[1]

    return pl.pallas_call(
        kernel,
        out_shape=[pltpu.VMEM(x.shape, x.dtype) for x in (lowest, stats)],
        in_specs=[VMEM] * 3,
        out_specs=[VMEM] * 2,
        input_output_aliases={0: 0, 2: 1},
        compiler_params=GRANT,
        name="pack",
    )(*near(lowest, right, stats))


def outer(now, basis, above, right, stats, lowest, coarse, *small):
    count = above.shape[0] // 2
    shape = jax.ShapeDtypeStruct((2, count), jnp.float32)
    return pl.pallas_call(
        lambda *refs: outer_kernel(count, now, *refs),
        out_shape=(whole(count), shape, shape, pltpu.VMEM(lowest.shape, lowest.dtype)),
        in_specs=[VMEM] * 5 + [ANY] * (1 + len(small)),
        out_specs=(ANY, ANY, ANY, VMEM),
        input_output_aliases={4: 3, 5: 0} | {6 + k: 1 + k for k in range(len(small))},
        scratch_shapes=scratch(count) + [pltpu.VMEM((2, 2, count), jnp.float32), pltpu.SemaphoreType.DMA((2,))],
        compiler_params=GRANT,
        name="outer",
    )(*near(basis, above, right, stats, lowest), coarse, *small)


def pull(x, dx, dy, takes=lambda h: True):
    nx, ny = lax.axis_size("gx"), lax.axis_size("gy")
    pairs = [((g + dx) % nx * ny + (h + dy) % ny, g * ny + h) for g in range(nx) for h in range(ny) if takes(h)]
    return lax.ppermute(x, ("gx", "gy"), pairs)


def body(site_tensors, test_matrix):
    columns, rows = lax.axis_size("gx"), lax.axis_size("gy")
    half = 17 if rows > 17 else max(1, rows // 2)
    g = lambda: lax.axis_index("gx")
    h = lambda: lax.axis_index("gy")
    ahead = lambda: (h() == 0) & (g() == columns - 1)
    leftmost, tensors, tests = split_left(site_tensors, test_matrix)
    right = pull(leftmost, 1, 0)
    basis, second, lowest = split_block(tensors, tests)
    coarse, stats = inner("ahead", ahead, basis, second)
    lowest, stats = pack(lowest, right, stats)
    near_above = pull(lowest, 0, 1, lambda h: h < half)
    coarse, stats = inner("near", lambda: jnp.logical_not(ahead()) & (h() < half), basis, second, coarse, stats)
    coarse, log_norm, trace, lowest = outer(lambda: h() < half, basis, near_above, right, stats, lowest, coarse)
    far_above = pull(lowest, 0, 1, lambda h: h >= half)
    coarse, stats = inner("far", lambda: h() >= half, basis, second, coarse, stats)
    coarse, log_norm, trace, _ = outer(
        lambda: h() >= half, basis, far_above, right, stats, lowest, coarse, log_norm, trace
    )
    return coarse, log_norm.T, trace.T


def solution(mesh):
    in_specs = (P("gx", "gy", None, None), P("gx", "gy", None, None))
    out_specs = (P("gx", "gy", None, None), P("gx", "gy"), P("gx", "gy"))
    return jax.shard_map(body, mesh=mesh, in_specs=in_specs, out_specs=out_specs, check_vma=False)
```

```python
import jax
import jax.numpy as jnp
from jax import lax
from jax.experimental import pallas as pl
from jax.experimental.pallas import tpu as pltpu
from jax.sharding import PartitionSpec as P

CHI = 16
WIDE = CHI * CHI
HALF = 128
NT = (((1,), (1,)), ((), ()))
NN = (((1,), (0,)), ((), ()))


ANY = pl.BlockSpec(memory_space=pl.ANY)
VMEM = pl.BlockSpec(memory_space=pltpu.VMEM)
GRANT = pltpu.CompilerParams(vmem_limit_bytes=32 << 20)


def near(*arrays):
    return [pltpu.with_memory_space_constraint(x, pltpu.VMEM) for x in arrays]


def dot(a, b, dims=NN):
    return lax.dot_general(a, b, dims, preferred_element_type=jnp.float32)


def split_sites(sources, slots, work):
    count = len(sources)
    for s, (test, tensor) in enumerate(sources):
        sketch = dot(test[...], tensor[...], NT)
        for slot in range(s, slots, count):
            for h in range(2):
                work[h, pl.ds(slot, CHI, stride=slots), :] = sketch[:, h * HALF : (h + 1) * HALF]

    def line(h, k):
        return work[h, k * slots : (k + 1) * slots, :]

    def inner(i, j):
        parts = line(0, i) * line(0, j) + line(1, i) * line(1, j)
        return jnp.broadcast_to(jnp.sum(parts, axis=1, keepdims=True), (slots, HALF))

    gram = {(i, j): inner(i, j) for j in range(CHI) for i in range(j, CHI)}
    for k in range(CHI):
        scale = lax.rsqrt(gram[k, k])
        lower = {i: gram[i, k] * scale for i in range(k + 1, CHI)}
        for i in range(k + 1, CHI):
            for j in range(k + 1, i + 1):
                gram[i, j] = gram[i, j] - lower[i] * lower[j]
        for h in range(2):
            row = line(h, k) * scale
            work[h, k * slots : (k + 1) * slots, :] = row
            for i in range(k + 1, CHI):
                work[h, i * slots : (i + 1) * slots, :] = line(h, i) - lower[i] * row
    for s, (_, tensor) in enumerate(sources):
        halves = [work[h, pl.ds(s, CHI, stride=slots), :] for h in range(2)]
        basis = jnp.concatenate(halves, axis=1).astype(jnp.bfloat16)
        yield s, basis, dot(basis, tensor[...]).astype(jnp.bfloat16)


def left_kernel(columns, rows, tensors, tests, leftmost, vm, vt, work, sem):
    copies = []
    for k, part in enumerate((pl.ds(0, 1), pl.ds(1, columns - 1))):
        copies.append(pltpu.make_async_copy(tests.at[part], vt.at[part], sem.at[0, k]))
        copies.append(pltpu.make_async_copy(tensors.at[part], vm.at[part], sem.at[1, k]))
    for copy in copies:
        copy.start()
    for copy in copies[:2]:
        copy.wait()
    for y, basis, second in split_sites([(vt.at[0, y], vm.at[0, y]) for y in range(rows)], 8, work):
        leftmost[1 - y] = basis if y == 1 else second
    for copy in copies[2:]:
        copy.wait()


def split_kernel(columns, rows, tensors, tests, basis, second, lowest, work):
    place = [(x, y) for x in range(columns) for y in range(rows)]
    for s, one, other in split_sites([(tests.at[x, y], tensors.at[x, y]) for x, y in place], len(place), work):
        x, y = place[s]
        basis[x, y] = one
        if y == 1:
            second[x] = other
        elif x > 0:
            lowest[x - 1] = other


def split_left(tensors, tests):
    columns, rows = tensors.shape[0], tensors.shape[1]
    return pl.pallas_call(
        lambda *refs: left_kernel(columns, rows, *refs),
        out_shape=[
            pltpu.VMEM((2, CHI, WIDE), jnp.bfloat16),
            pltpu.VMEM(tensors.shape, tensors.dtype),
            pltpu.VMEM(tests.shape, tests.dtype),
        ],
        in_specs=[ANY] * 2,
        out_specs=[VMEM] * 3,
        scratch_shapes=[pltpu.VMEM((2, CHI * 8, HALF), jnp.float32), pltpu.SemaphoreType.DMA((2, 2))],
        compiler_params=GRANT,
        name="split_left",
    )(*[pltpu.with_memory_space_constraint(x, pltpu.HBM) for x in (tensors, tests)])


def split_block(tensors, tests):
    columns, rows = tensors.shape[0], tensors.shape[1]
    shapes = [(columns, rows), (columns,), (columns,)]
    return pl.pallas_call(
        lambda *refs: split_kernel(columns, rows, *refs),
        out_shape=[pltpu.VMEM(shape + (CHI, WIDE), jnp.bfloat16) for shape in shapes],
        in_specs=[VMEM] * 2,
        out_specs=[VMEM] * 3,
        scratch_shapes=[pltpu.VMEM((2, CHI * columns * rows, HALF), jnp.float32)],
        compiler_params=GRANT,
        name="split",
    )(*near(tensors, tests))


def widen(half, pick, tile):
    spread = jnp.broadcast_to(half.astype(jnp.float32)[:, None, :], (CHI, CHI, WIDE)).reshape(WIDE, WIDE)
    spread = jnp.where(pick, spread, 0.0).astype(jnp.bfloat16)
    return dot(spread, tile).astype(jnp.bfloat16)


def pair_up(wide, other, own, out):
    left = jnp.concatenate([other[:, :HALF], other[:, HALF:]], axis=0)
    for a in range(0, CHI, 2):
        blocks = []
        for step in range(2):
            piece = wide[(a + step) * CHI : (a + step + 1) * CHI, :]
            zero = jnp.zeros_like(piece)
            blocks.append(jnp.concatenate([jnp.where(own[v], piece, zero) for v in range(8)], axis=0))
        got = dot(left, jnp.concatenate(blocks, axis=1)).astype(jnp.bfloat16)
        for step in range(2):
            base = (a + step) * CHI
            for h in range(2):
                out[base : base + CHI, h * HALF : (h + 1) * HALF] = got[
                    h * CHI : (h + 1) * CHI, step * HALF : (step + 1) * HALF
                ]


def patterns():
    iota = lambda shape, axis: lax.broadcasted_iota(jnp.int32, shape, axis)
    r, c = iota((WIDE, WIDE), 0), iota((WIDE, WIDE), 1)
    rt, ct = iota((WIDE, HALF), 0), iota((WIDE, HALF), 1)
    lane = iota((CHI, HALF), 1)
    return dict(
        pick_minor=(c % CHI) == (r % CHI),
        pick_major=(c // CHI) == (r % CHI),
        tile_major=((rt // CHI) == (ct % CHI)).astype(jnp.float32).astype(jnp.bfloat16),
        tile_minor=((rt % CHI) == (ct % CHI)).astype(jnp.float32).astype(jnp.bfloat16),
        own=[(lane // CHI) == v for v in range(8)],
        crossed=((c // CHI) == (r % CHI)) & ((c % CHI) == (r // CHI)),
        small=(iota((8, HALF), 0), iota((8, HALF), 1)),
    )


def contract_row(row, count, corners, coarse, stats, low, high, done, sem):
    at = patterns()
    rows, lanes = at["small"]
    copies = []
    pairs = []
    for p in range(count):
        north_east, north_west, south_east, south_west = corners(p)
        pairs.append((widen(north_east, at["pick_minor"], at["tile_major"]), north_west, low.at[p]))
        pairs.append((widen(south_east, at["pick_major"], at["tile_minor"]), south_west, high.at[p]))
    for wide, other, out in pairs:
        pair_up(wide, other, at["own"], out)
    products = [dot(low[p], high[p], NT) for p in range(count)]
    for p, raw in enumerate(products):
        square = jnp.sum(jnp.sum(raw * raw, axis=0, keepdims=True), axis=1, keepdims=True) + 1e-06
        scale = lax.rsqrt(square)
        done[p] = (raw * (CHI * CHI * scale)).astype(jnp.bfloat16)
        copy = pltpu.make_async_copy(done.at[p], coarse.at[p, row], sem.at[p])
        copy.start()
        copies.append(copy)
        diagonal = jnp.where(at["crossed"], raw, 0.0)
        traced = jnp.sum(jnp.sum(diagonal, axis=0, keepdims=True), axis=1, keepdims=True)
        stats = jnp.where((rows == row) & (lanes == p), 0.5 * jnp.log(square), stats)
        stats = jnp.where((rows == 2 + row) & (lanes == p), CHI * traced * scale, stats)
    return stats, copies


def inner_kernel(count, kind, now, basis, second, *refs):
    stats_in = None
    if kind == "ahead":
        coarse, stats, low, high, done, sem = refs
    else:
        _, stats_in, coarse, stats, low, high, done, sem = refs

    def corners(p):
        return basis[2 * p, 0], basis[2 * p + 1, 0], second[2 * p], second[2 * p + 1]

    here = now()

    @pl.when(here)
    def _():
        got, copies = contract_row(0, count, corners, coarse, jnp.zeros((8, HALF), jnp.float32), low, high, done, sem)
        stats[...] = got
        for copy in copies:
            copy.wait()

    @pl.when(jnp.logical_not(here))
    def _():
        stats[...] = jnp.zeros((8, HALF), jnp.float32) if stats_in is None else stats_in[...]


def outer_kernel(count, now, basis, above, right, stats_in, *refs):
    coarse, logs, traces, _, low, high, done, sem, vs, sem_s = refs[-10:]

    def corners(p):
        beside = basis[2 * p + 2, 1] if p < count - 1 else right[0]
        return basis[2 * p + 1, 1], beside, above[2 * p], above[2 * p + 1]

    @pl.when(now())
    def _():
        stats, copies = contract_row(1, count, corners, coarse, stats_in[...], low, high, done, sem)
        vs[0] = stats[0:2, :count]
        vs[1] = stats[2:4, :count]
        small = [pltpu.make_async_copy(vs.at[0], logs, sem_s.at[0]), pltpu.make_async_copy(vs.at[1], traces, sem_s.at[1])]
        for copy in small:
            copy.start()
        for copy in copies + small:
            copy.wait()


def scratch(count):
    return [
        pltpu.VMEM((count, WIDE, WIDE), jnp.bfloat16),
        pltpu.VMEM((count, WIDE, WIDE), jnp.bfloat16),
        pltpu.VMEM((count, WIDE, WIDE), jnp.bfloat16),
        pltpu.SemaphoreType.DMA((count,)),
    ]


def whole(count):
    return jax.ShapeDtypeStruct((count, 2, WIDE, WIDE), jnp.bfloat16)


def inner(kind, now, basis, second, *before):
    count = second.shape[0] // 2
    return pl.pallas_call(
        lambda *refs: inner_kernel(count, kind, now, *refs),
        out_shape=(whole(count), pltpu.VMEM((8, HALF), jnp.float32)),
        in_specs=[VMEM, VMEM, ANY, VMEM][: 2 + len(before)],
        out_specs=(ANY, VMEM),
        input_output_aliases={2: 0} if before else {},
        scratch_shapes=scratch(count),
        compiler_params=GRANT,
        name="inner_" + kind,
    )(*near(basis, second), *before[:1], *near(*before[1:]))


def pack(lowest, right, stats):
    def kernel(lowest_in, right_in, stats_in, lowest_out, stats_out):
        lowest_out[lowest.shape[0] - 1] = right_in[1]

    return pl.pallas_call(
        kernel,
        out_shape=[pltpu.VMEM(x.shape, x.dtype) for x in (lowest, stats)],
        in_specs=[VMEM] * 3,
        out_specs=[VMEM] * 2,
        input_output_aliases={0: 0, 2: 1},
        compiler_params=GRANT,
        name="pack",
    )(*near(lowest, right, stats))


def outer(now, basis, above, right, stats, lowest, coarse, *small):
    count = above.shape[0] // 2
    shape = jax.ShapeDtypeStruct((2, count), jnp.float32)
    return pl.pallas_call(
        lambda *refs: outer_kernel(count, now, *refs),
        out_shape=(whole(count), shape, shape, pltpu.VMEM(lowest.shape, lowest.dtype)),
        in_specs=[VMEM] * 5 + [ANY] * (1 + len(small)),
        out_specs=(ANY, ANY, ANY, VMEM),
        input_output_aliases={4: 3, 5: 0} | {6 + k: 1 + k for k in range(len(small))},
        scratch_shapes=scratch(count) + [pltpu.VMEM((2, 2, count), jnp.float32), pltpu.SemaphoreType.DMA((2,))],
        compiler_params=GRANT,
        name="outer",
    )(*near(basis, above, right, stats, lowest), coarse, *small)


def pull(x, dx, dy, takes=lambda h: True):
    nx, ny = lax.axis_size("gx"), lax.axis_size("gy")
    pairs = [((g + dx) % nx * ny + (h + dy) % ny, g * ny + h) for g in range(nx) for h in range(ny) if takes(h)]
    return lax.ppermute(x, ("gx", "gy"), pairs)


def body(site_tensors, test_matrix):
    columns, rows = lax.axis_size("gx"), lax.axis_size("gy")
    half = 17 if rows > 17 else max(1, rows // 2)
    g = lambda: lax.axis_index("gx")
    h = lambda: lax.axis_index("gy")
    ahead = lambda: (h() == 0) & (g() == columns - 1)
    leftmost, tensors, tests = split_left(site_tensors, test_matrix)
    right = pull(leftmost, 1, 0)
    basis, second, lowest = split_block(tensors, tests)
    coarse, stats = inner("ahead", ahead, basis, second)
    lowest, stats = pack(lowest, right, stats)
    near_above = pull(lowest, 0, 1, lambda h: h < half)
    coarse, stats = inner("near", lambda: jnp.logical_not(ahead()) & (h() < half), basis, second, coarse, stats)
    coarse, log_norm, trace, lowest = outer(lambda: h() < half, basis, near_above, right, stats, lowest, coarse)
    far_above = pull(lowest, 0, 1, lambda h: h >= half)
    coarse, stats = inner("far", lambda: h() >= half, basis, second, coarse, stats)
    coarse, log_norm, trace, _ = outer(
        lambda: h() >= half, basis, far_above, right, stats, lowest, coarse, log_norm, trace
    )
    return coarse, log_norm.T, trace.T


def solution(mesh):
    in_specs = (P("gx", "gy", None, None), P("gx", "gy", None, None))
    out_specs = (P("gx", "gy", None, None), P("gx", "gy"), P("gx", "gy"))
    return jax.shard_map(body, mesh=mesh, in_specs=in_specs, out_specs=out_specs, check_vma=False)
```
